32 devices in a mesh: seq: 16 (over z, y, x), head: 2 (over core).
Axes of the slice: x: 2, y: 2, z: 4, core: 2. Of those that a mesh axis runs over, the one named last changes fastest.
Arguments:
- x_inner: bfloat16 [2, 8192, 5120], P(None, 'seq', 'head'), may hold values from -6 to 6
- z_gate: bfloat16 [2, 8192, 5120], P(None, 'seq', 'head'), may hold values from -200 to 200
- b_input: bfloat16 [2, 8192, 128], P(None, 'seq'), may hold values from -6 to 6
- c_output: bfloat16 [2, 8192, 128], P(None, 'seq'), may hold values from -6 to 6
- step_sizes: float32 [2, 8192, 80], P(None, 'seq', 'head'), may hold values from 0.0002 to 0.2
- decay_log: float32 [80], P('head'), may hold values from -20 to 2
- skip_gain: float32 [80], P('head'), may hold values from 1 to 4
- norm_gain: float32 [5120], P('head'), may hold values from 0.5 to 1.5
- goal_pos: int32 [2, 512], P(None, 'seq'), may hold values from 0 to 8191, as said below
- goal_owner: int32 [2, 512], P(None, 'seq'), may hold values from 0 to 15, as said below
- value_w1: bfloat16 [16, 5120, 1024], P('seq', None, 'head'), may hold values from -0.078125 to 0.078125
- value_b1: float32 [16, 1024], P('seq', 'head'), may hold values from -3 to 3
- value_w2: bfloat16 [16, 1024], P('seq', 'head'), may hold values from -0.1875 to 0.1875
Outputs:
- layer_out: bfloat16 [2, 8192, 5120], P(None, 'seq', 'head')
- values: float32 [2, 512], P(None, 'seq')
The draws below stay inside these ranges and needn't reach their ends.
Inputs may be any that keep to these rules, and one draw needn't show every extreme that they name: For every sequence s and every b, goal_pos[s, b * 32 + i] for i < 32 are distinct positions from b * 512 to (b + 1) * 512 - 1, increasing in i. `goal_owner`: among the 2 x 32 goals of the columns b * 32 to (b + 1) * 32 - 1, no expert is named more than 4 times; one expert is named exactly 4 times in every such group of columns.
All inputs are finite; a program needn't handle non-finite values.
Results may differ from the reference program's by a relative error of at most 0.0056.
Values may be sent and summed in bfloat16 or wider, within the bound.
No kernel may reach another device: no remote copies, remote signals or barrier semaphores. Data moves between devices by JAX's collectives and lax.ppermute only.
A program may use at most 384 MiB of HBM per device.

```python
from functools import partial
import jax
import jax.numpy as jnp
from jax import lax

HEAD_TOTAL = 80
HEAD_DIM = 64
NSTATE = 128
BLOCK = 256
VH = 1024
SEQUENCE_TOTAL = 2
TOK_DEV = 512
GOAL_DEV = 32
CAP = 4
LEN = 8192
GOALS = 512
VALUE_EXPERTS = 16


def head_classes(key):
    class_key = jax.random.fold_in(key, 101)
    slow_share = 0.5
    return jax.random.uniform(class_key, (HEAD_TOTAL,)) < slow_share


def draw_decay_log(key, part):
    slow_heads = head_classes(key)
    first_key, second_key = jax.random.split(jax.random.fold_in(key, 202))
    slow_rate = jnp.exp(jax.random.uniform(first_key, (HEAD_TOTAL,), minval=jnp.log(0.5), maxval=0.0)) / (LEN * 0.00211)
    fast_rate = jnp.exp(jax.random.uniform(second_key, (HEAD_TOTAL,), minval=jnp.log(0.5), maxval=jnp.log(0.9)))
    return jnp.log(jnp.where(slow_heads, slow_rate, fast_rate)).astype(jnp.float32)


def draw_step_sizes(key, part):
    slow_heads = head_classes(key)
    base_random_key, block_random_key, spike_random_key = jax.random.split(jax.random.fold_in(key, 303), 3)
    factor_key = jax.random.fold_in(key, 707)
    base_steps = jnp.exp(jax.random.uniform(base_random_key, (SEQUENCE_TOTAL, LEN, HEAD_TOTAL), minval=jnp.log(0.001), maxval=jnp.log(0.004)))
    block_factor = jnp.exp(jax.random.uniform(block_random_key, (SEQUENCE_TOTAL, LEN // TOK_DEV, 1, HEAD_TOTAL), minval=jnp.log(0.5), maxval=jnp.log(2.0)))
    base_steps = (base_steps.reshape(SEQUENCE_TOTAL, LEN // TOK_DEV, TOK_DEV, HEAD_TOTAL) * block_factor).reshape(SEQUENCE_TOTAL, LEN, HEAD_TOTAL)
    block_number = LEN // BLOCK
    spike_blocks = jax.random.randint(spike_random_key, (SEQUENCE_TOTAL, 2, HEAD_TOTAL), 0, block_number)
    position_to_block = jnp.arange(LEN, dtype=jnp.int32) // BLOCK
    inside_spike = jnp.any(position_to_block[None, None, :, None] == spike_blocks[:, :, None, :], axis=1)
    spike_factor = 0.19 * block_number
    slowdown_factor = jnp.where(inside_spike, spike_factor, 1.0)
    fast_factor = jnp.exp(jax.random.uniform(factor_key, (HEAD_TOTAL,), minval=0.0, maxval=jnp.log(20.0)))
    head_factor = jnp.where(slow_heads[None, None, :], slowdown_factor, fast_factor[None, None, :])
    return (base_steps * head_factor).astype(jnp.float32)


def draw_z_gate(key, part):
    width_total = HEAD_TOTAL * HEAD_DIM
    noise_key, column_key, row_key = jax.random.split(jax.random.fold_in(key, 404), 3)
    random_jitter = jax.random.normal(noise_key, (SEQUENCE_TOTAL, LEN, width_total))
    column_ramp = jnp.power(10.0, jnp.arange(width_total, dtype=jnp.float32) / width_total)
    column_scale = column_ramp * jnp.exp(jax.random.uniform(column_key, (width_total,), minval=jnp.log(0.7), maxval=jnp.log(1.4)))
    row_scale = jnp.exp(jax.random.uniform(row_key, (SEQUENCE_TOTAL, LEN, 1), minval=jnp.log(0.5), maxval=jnp.log(2.0)))
    return (0.5 * random_jitter * column_scale * row_scale).astype(jnp.float32).astype(jnp.bfloat16)


def draw_goal_pos(key, part):
    block_number = LEN // TOK_DEV
    block_keys = jax.random.split(jax.random.fold_in(key, 505), SEQUENCE_TOTAL * block_number)

    def one_block(block_random_key):
        picked = jnp.sort(jax.random.permutation(block_random_key, TOK_DEV)[:GOAL_DEV])
        return picked.at[0].set(0).at[GOAL_DEV - 1].set(TOK_DEV - 1)
    offsets = jax.vmap(one_block)(block_keys).reshape(SEQUENCE_TOTAL, block_number, GOAL_DEV)
    starts = (jnp.arange(block_number, dtype=jnp.int32) * TOK_DEV)[None, :, None]
    return (offsets + starts).reshape(SEQUENCE_TOTAL, GOALS).astype(jnp.int32)


def draw_goal_owner(key, part):
    popular_expert_key, extra_score_key, remainder_key = jax.random.split(jax.random.fold_in(key, 606), 3)
    hot_expert = jax.random.randint(popular_expert_key, (), 0, VALUE_EXPERTS)
    extra_score = jax.random.randint(extra_score_key, (VALUE_EXPERTS,), 0, 4)
    block_number = LEN // TOK_DEV
    per_block = SEQUENCE_TOTAL * GOAL_DEV
    slot_number = VALUE_EXPERTS * CAP
    slot_numbers = jnp.arange(slot_number, dtype=jnp.int32)
    expert_per_slot = slot_numbers // CAP

    def one_block(block_random_key):
        score_key, order_key = jax.random.split(block_random_key)
        random_jitter = jax.random.randint(score_key, (slot_number,), 0, 4096)
        routing_scores = (extra_score[expert_per_slot] * 1024 + random_jitter) * slot_number + slot_numbers
        routing_scores = jnp.where(expert_per_slot == hot_expert, -1, routing_scores)
        chosen = lax.top_k(routing_scores, per_block - CAP)[1]
        named = jnp.concatenate([jnp.full((CAP,), hot_expert, jnp.int32), expert_per_slot[chosen].astype(jnp.int32)])
        return jax.random.permutation(order_key, named)
    owners = jax.vmap(one_block)(jax.random.split(remainder_key, block_number))
    return jnp.transpose(owners.reshape(block_number, SEQUENCE_TOTAL, GOAL_DEV), (1, 0, 2)).reshape(SEQUENCE_TOTAL, GOALS).astype(jnp.int32)


def levels(key, dims, cuts, least, largest):
    def one(position, parts):
        draws = jax.random.uniform(jax.random.fold_in(jax.random.fold_in(key, 6), position), (parts,), jnp.float32, least / len(cuts), largest / len(cuts))
        return jnp.repeat(jnp.exp(draws), dims[position] // parts).reshape((-1,) + (1,) * (len(dims) - position - 1))

    loudness = one(*cuts[0])
    for cut in cuts[1:]:
        loudness = loudness * one(*cut)
    return loudness


def normal_values(stream_key, dims, deviation, bound, cuts=(), kind=jnp.bfloat16):
    result = deviation * jax.random.normal(stream_key, dims, jnp.float32)
    if cuts:
        result = result * levels(stream_key, dims, cuts, -0.22, 0.18)
    return jnp.clip(result, -bound, bound).astype(kind)


def setup_inputs(seed: int = 0) -> dict:
    key_list = jax.random.split(jax.random.key(seed), 14)
    x_inner = normal_values(key_list[0], (SEQUENCE_TOTAL, LEN, HEAD_TOTAL * HEAD_DIM), 1.0, 6.0, ((1, 16), (2, 2)))
    z_gate = draw_z_gate(jax.random.fold_in(key_list[13], 71), 0)
    b_input = normal_values(key_list[2], (SEQUENCE_TOTAL, LEN, NSTATE), 1.0, 6.0, ((1, 16),))
    c_output = normal_values(key_list[3], (SEQUENCE_TOTAL, LEN, NSTATE), 1.0, 6.0, ((1, 16),))
    step_sizes = draw_step_sizes(jax.random.fold_in(key_list[13], 71), 0)
    decay_log = draw_decay_log(jax.random.fold_in(key_list[13], 71), 0)
    skip_gain = jnp.clip(1.0 + 3.0 * jax.random.uniform(key_list[6], (HEAD_TOTAL,), jnp.float32) ** levels(key_list[6], (HEAD_TOTAL,), ((0, 2),), -0.2, 0.2), 1.0, 4.0)
    norm_gain = jnp.clip(1.0 + 0.1 * jax.random.normal(key_list[7], (HEAD_TOTAL * HEAD_DIM,), jnp.float32), 0.5, 1.5)
    goal_pos = draw_goal_pos(jax.random.fold_in(key_list[13], 71), 0)
    goal_owner = draw_goal_owner(jax.random.fold_in(key_list[13], 71), 0)
    value_w1 = normal_values(key_list[10], (VALUE_EXPERTS, HEAD_TOTAL * HEAD_DIM, VH), (HEAD_TOTAL * HEAD_DIM) ** -0.5, 0.078125, ((0, 16), (2, 2)))
    value_b1 = normal_values(key_list[11], (VALUE_EXPERTS, VH), 0.5, 3.0, ((0, 16), (1, 2)), jnp.float32)
    value_w2 = normal_values(key_list[12], (VALUE_EXPERTS, VH), VH ** -0.5, 0.1875, ((0, 16), (1, 2)))
    return dict(x_inner=x_inner, z_gate=z_gate, b_input=b_input, c_output=c_output, step_sizes=step_sizes, decay_log=decay_log, skip_gain=skip_gain, norm_gain=norm_gain, goal_pos=goal_pos, goal_owner=goal_owner, value_w1=value_w1, value_b1=value_b1, value_w2=value_w2)


norm_eps = 1e-05

def rounded(value):
    return lax.optimization_barrier(value.astype(jnp.bfloat16)).astype(jnp.float32)

def block_step(state_in, inputs, decay_rates, skip_heads):
    x_piece, b_piece, c_piece, dt_piece = inputs
    head_count = dt_piece.shape[1]
    x_float = x_piece.reshape(BLOCK, head_count, -1).astype(jnp.float32)
    cumulative = jnp.cumsum(dt_piece * decay_rates[None, :], axis=0).T
    dt_heads = dt_piece.T
    routing_scores = jnp.dot(c_piece, b_piece.T, preferred_element_type=jnp.float32)
    positions = jnp.arange(BLOCK)
    lower_mask = positions[:, None] >= positions[None, :]
    spread = cumulative[:, :, None] - cumulative[:, None, :]
    decay_mat = jnp.exp(jnp.where(lower_mask[None], spread, -jnp.inf))
    weights = rounded(routing_scores[None] * decay_mat * dt_heads[:, None, :])
    y_diag = jnp.einsum('hkr,rhp->khp', weights, x_float)
    carried = rounded(state_in)
    y_off = jnp.einsum('kn,hpn->khp', c_piece.astype(jnp.float32), carried) * jnp.exp(cumulative.T)[:, :, None]
    y_all = y_diag + y_off + skip_heads[None, :, None] * x_float
    end_weights = jnp.exp(cumulative[:, -1:] - cumulative) * dt_heads
    x_weighted = rounded(x_float * end_weights.T[:, :, None])
    states = jnp.einsum('rhp,rn->hpn', x_weighted, b_piece.astype(jnp.float32))
    new_state = jnp.exp(cumulative[:, -1])[:, None, None] * state_in + states
    return (new_state, y_all.reshape(BLOCK, -1))

def pick_rows(layer_seq, index_seq):
    return jnp.take(layer_seq, index_seq, axis=0)

def reference(x_inner, z_gate, b_input, c_output, step_sizes, decay_log, skip_gain, norm_gain, goal_pos, goal_owner, value_w1, value_b1, value_w2):
    decay_rates = -jnp.exp(decay_log)
    block_count = LEN // BLOCK
    outputs = []
    for seq_index in range(SEQUENCE_TOTAL):
        pieces = (x_inner[seq_index].reshape(block_count, BLOCK, -1), b_input[seq_index].reshape(block_count, BLOCK, -1), c_output[seq_index].reshape(block_count, BLOCK, -1), step_sizes[seq_index].reshape(block_count, BLOCK, -1))
        zero_state = jnp.zeros((HEAD_TOTAL, HEAD_DIM, NSTATE), jnp.float32)
        final_state, block_outs = lax.scan(partial(block_step, decay_rates=decay_rates, skip_heads=skip_gain), zero_state, pieces)
        outputs.append(block_outs.reshape(LEN, -1))
    y_full = jnp.stack(outputs)
    gated_out = y_full * jax.nn.silu(z_gate.astype(jnp.float32))
    inv_rms = lax.rsqrt(lax.optimization_barrier(jnp.mean(gated_out * gated_out, axis=-1, keepdims=True)) + norm_eps)
    layer_out = (gated_out * inv_rms * norm_gain).astype(jnp.bfloat16)
    picked_rows = jax.vmap(pick_rows)(layer_out, goal_pos).reshape(SEQUENCE_TOTAL * GOALS, -1)
    owners = goal_owner.reshape(-1)

    def one_value(item):
        goal_row, owner_id = item
        hidden = jnp.dot(goal_row, value_w1[owner_id], preferred_element_type=jnp.float32) + value_b1[owner_id]
        hidden = jax.nn.gelu(hidden).astype(jnp.bfloat16)
        return jnp.dot(hidden, value_w2[owner_id], preferred_element_type=jnp.float32)
    values = lax.map(one_value, (picked_rows, owners)).reshape(SEQUENCE_TOTAL, GOALS)
    return (layer_out, values)
```

```python
import functools

import jax
import jax.numpy as jnp
import numpy as np
from jax import lax
from jax.experimental import pallas as pl
from jax.experimental.pallas import tpu as pltpu
from jax.sharding import PartitionSpec as P

HEAD_TOTAL = 80
HEAD_DIM = 64
NSTATE = 128
CAP = 4
PLANES = 4
CHUNK = 128
TILE = 256
EXTRA = 128
LOG2E = 1.4426950408889634
norm_eps = 1e-05
F32 = jnp.float32
BF16 = jnp.bfloat16
HIGHEST = lax.Precision.HIGHEST


def mm(a, b):
    return jnp.dot(a, b, preferred_element_type=F32)


def lane_parts(v, heads):
    hi = v.astype(BF16)
    rest = v - hi.astype(F32)
    mid = rest.astype(BF16)
    lo = (rest - mid.astype(F32)).astype(BF16)
    lane = lax.broadcasted_iota(jnp.int32, v.shape, 1)
    return jnp.where(
        lane < heads, hi.astype(F32), jnp.where(lane < 2 * heads, mid.astype(F32), lo.astype(F32))
    ).astype(BF16)


def three(v):
    hi = v.astype(BF16).astype(F32)
    mid = (v - hi).astype(BF16).astype(F32)
    return hi, mid, v - hi - mid


def tri_mask():
    rows = lax.broadcasted_iota(jnp.int32, (CHUNK, CHUNK), 0)
    cols = lax.broadcasted_iota(jnp.int32, (CHUNK, CHUNK), 1)
    return rows >= cols


def summary_kernel(groups, heads, me, x, b, dt, rate, spread, *rest):
    outs, (cum, parts, bt, st) = rest[:groups], rest[groups:]
    step = pl.program_id(0)
    length = dt.shape[1]
    width = x.shape[2]
    rows = NSTATE // groups

    @pl.when(step == 0)
    def _():
        tri = tri_mask().astype(F32)
        before = jnp.zeros((1, 128), F32)
        for k in range(length // CHUNK):
            at = pl.ds(k * CHUNK, CHUNK)
            part = (
                jnp.dot(tri, dt[0, at, :] * rate[...], precision=HIGHEST, preferred_element_type=F32)
                + before
            )
            cum[at, :] = part
            before = part[CHUNK - 1 :, :]
            bt[:, at] = b[0, at, :].astype(F32).T.astype(BF16)
        for k in range(length // CHUNK):
            at = pl.ds(k * CHUNK, CHUNK)
            parts[at, :] = lane_parts(jnp.exp2(before - cum[at, :]) * dt[0, at, :], heads)
        hi, mid, lo = three(before)
        row = lax.broadcasted_iota(jnp.int32, (rows, EXTRA), 0)
        extra = jnp.where(row == 0, hi, jnp.where(row == 1, mid, jnp.where(row == 2, lo, 0.0)))
        for d in range(groups):
            outs[d][:, pl.ds(outs[d].shape[1] - EXTRA, EXTRA)] = extra.astype(BF16)

    for i in range(width // TILE):
        at = pl.ds(i * TILE, TILE)
        weighted = (x[0, :, at].astype(F32) * mm(parts[...], spread[:, at])).astype(BF16)
        st[:, at] = mm(bt[...], weighted)
    for d in range(groups):
        outs[d][:, pl.ds(pl.multiple_of(step * width, 128), width)] = st[
            pl.ds(pl.multiple_of((me[0] ^ d) * rows, 8), rows), :
        ].astype(BF16)


def summary(s, me, x, b, dt, rate, spread, groups):
    length, feats = x.shape[1:]
    width = 512
    heads = feats // HEAD_DIM
    return pl.pallas_call(
        functools.partial(summary_kernel, groups, heads),
        grid_spec=pltpu.PrefetchScalarGridSpec(
            num_scalar_prefetch=1,
            grid=(feats // width,),
            in_specs=[
                pl.BlockSpec((1, length, width), lambda i, m: (s, 0, i)),
                pl.BlockSpec((1, length, NSTATE), lambda i, m: (s, 0, 0)),
                pl.BlockSpec((1, length, 128), lambda i, m: (s, 0, 0)),
                pl.BlockSpec((1, 128), lambda i, m: (0, 0)),
                pl.BlockSpec((128, width), lambda i, m: (0, i)),
            ],
            out_specs=[pl.BlockSpec((NSTATE // groups, feats + EXTRA), lambda i, m: (0, 0))] * groups
            + [pl.BlockSpec((length, 128), lambda i, m: (0, 0))],
            scratch_shapes=[
                pltpu.VMEM((length, 128), BF16),
                pltpu.VMEM((NSTATE, length), BF16),
                pltpu.VMEM((NSTATE, width), F32),
            ],
        ),
        out_shape=[jax.ShapeDtypeStruct((NSTATE // groups, feats + EXTRA), BF16)] * groups
        + [jax.ShapeDtypeStruct((length, 128), F32)],
        compiler_params=pltpu.CompilerParams(vmem_limit_bytes=24 << 20),
        cost_estimate=pl.CostEstimate(flops=1_400_000_000, bytes_accessed=4_000_000, transcendentals=0),
        name="summary",
    )(me, x, b, dt, rate, spread)


def totals_of(pieces, feats):
    out = []
    for piece in pieces:
        block = piece[0:8, pl.ds(feats, EXTRA)].astype(F32)
        out.append(block[0:1] + block[1:2] + block[2:3])
    return out


def factors(totals, spread, heads, tile):
    fill = [jnp.zeros((1, 128), F32)] * (-len(totals) % 16)
    stacked = jnp.concatenate(totals + fill, axis=0)
    return mm(lane_parts(jnp.exp2(stacked), heads), spread[:, tile])


def plane_kernel(groups, heads, me, spread, *rest):
    pieces, out, ordered = rest[:groups], rest[groups], rest[groups + 1]
    feats = spread.shape[1]
    rows = out.shape[0]
    for d in range(groups):
        ordered[d] = pieces[d][...]
    views = [ordered.at[me[0] ^ p] for p in range(groups)]
    totals = totals_of(views, feats)
    for i in range(feats // TILE):
        at = pl.ds(i * TILE, TILE)
        decay = factors(totals, spread, heads, at)
        total = views[0][:, at].astype(F32)
        for p in range(1, groups):
            total = decay[p : p + 1] * total + views[p][:, at].astype(F32)
        out[:, at] = total.astype(BF16)
    hi, mid, lo = three(functools.reduce(lambda a, b: a + b, totals))
    row = lax.broadcasted_iota(jnp.int32, (rows, EXTRA), 0)
    extra = jnp.where(row == 0, hi, jnp.where(row == 1, mid, jnp.where(row == 2, lo, 0.0)))
    out[:, pl.ds(feats, EXTRA)] = extra.astype(BF16)


def plane_total(me, spread, pieces):
    groups = len(pieces)
    rows, wide = pieces[0].shape
    heads = spread.shape[1] // HEAD_DIM
    vmem = pl.BlockSpec(memory_space=pltpu.VMEM)
    return pl.pallas_call(
        functools.partial(plane_kernel, groups, heads),
        in_specs=[pl.BlockSpec(memory_space=pltpu.SMEM)] + [vmem] * (groups + 1),
        out_specs=vmem,
        out_shape=jax.ShapeDtypeStruct((rows, wide), BF16),
        scratch_shapes=[pltpu.VMEM((groups, rows, wide), BF16)],
        compiler_params=pltpu.CompilerParams(vmem_limit_bytes=16 << 20),
        cost_estimate=pl.CostEstimate(flops=10_000_000, bytes_accessed=1_500_000, transcendentals=0),
        name="plane_total",
    )(me, spread, *pieces)


def incoming_kernel(groups, hops, heads, me, spread, *rest):
    pieces, below = rest[:groups], rest[groups : groups + hops]
    outs = rest[groups + hops : 2 * groups + hops]
    ordered, results = rest[2 * groups + hops :]
    feats = spread.shape[1]
    for d in range(groups):
        ordered[d] = pieces[d][...]
    views = [ordered.at[me[0] ^ p] for p in range(groups)]
    totals = totals_of(views, feats)
    below_totals = totals_of(below, feats)
    for i in range(feats // TILE):
        at = pl.ds(i * TILE, TILE)
        decay = factors(totals + below_totals, spread, heads, at)
        state = jnp.zeros((pieces[0].shape[0], TILE), F32)
        for k in range(hops - 1, -1, -1):
            state = decay[groups + k : groups + k + 1] * state + below[k][:, at].astype(F32)
        for p in range(groups):
            results[me[0] ^ p, :, at] = state.astype(BF16)
            if p < groups - 1:
                state = decay[p : p + 1] * state + views[p][:, at].astype(F32)
    for d in range(groups):
        outs[d][...] = results[d]


def incoming_states(me, spread, pieces, below):
    groups, hops = len(pieces), len(below)
    rows, wide = pieces[0].shape
    feats = spread.shape[1]
    vmem = pl.BlockSpec(memory_space=pltpu.VMEM)
    return pl.pallas_call(
        functools.partial(incoming_kernel, groups, hops, feats // HEAD_DIM),
        in_specs=[pl.BlockSpec(memory_space=pltpu.SMEM)] + [vmem] * (1 + groups + hops),
        out_specs=[vmem] * groups,
        out_shape=[jax.ShapeDtypeStruct((rows, feats), BF16)] * groups,
        scratch_shapes=[
            pltpu.VMEM((groups, rows, wide), BF16),
            pltpu.VMEM((groups, rows, feats), BF16),
        ],
        compiler_params=pltpu.CompilerParams(vmem_limit_bytes=16 << 20),
        cost_estimate=pl.CostEstimate(flops=10_000_000, bytes_accessed=2_500_000, transcendentals=0),
        name="incoming_states",
    )(me, spread, *pieces, *below)


def local_kernel(heads, x, b, c, dt, rate, skip, spread, y, state, skip_wide):
    step = pl.program_id(0)
    feats = spread.shape[1]

    @pl.when(step == 0)
    def _():
        state[...] = jnp.zeros_like(state)
        for i in range(feats // TILE):
            at = pl.ds(i * TILE, TILE)
            skip_wide[:, at] = mm(
                lane_parts(jnp.broadcast_to(skip[...], (16, 128)), heads), spread[:, at]
            )[:8]

    keep = tri_mask()
    steps = dt[0]
    cum = jnp.dot(
        keep.astype(F32), steps * rate[...], precision=HIGHEST, preferred_element_type=F32
    )
    from_row = (cum - jnp.log2(steps)).T
    b_in, c_out = b[0], c[0]
    scores = lax.dot_general(c_out, b_in, (((1,), (1,)), ((), ())), preferred_element_type=F32)
    b_t = b_in.astype(F32).T.astype(BF16)
    grow = lane_parts(jnp.exp2(cum), heads)
    fade = lane_parts(jnp.exp2(cum[CHUNK - 1 :, :] - cum) * steps, heads)
    first = lax.broadcasted_iota(jnp.int32, (CHUNK, 128), 1) < HEAD_DIM
    nothing = jnp.zeros((CHUNK, 128), BF16)

    def weights(h):
        return jnp.where(
            keep, scores * jnp.exp2(cum[:, h : h + 1] - from_row[h : h + 1, :]), 0.0
        ).astype(BF16)

    for i in range(feats // TILE):
        at = pl.ds(i * TILE, TILE)
        grow_wide = mm(grow, spread[:, at])
        fade_wide = mm(fade, spread[:, at])
        x_in = x[0, :, at]
        x_float = x_in.astype(F32)
        old = state[:, at]
        y_tile = mm(c_out, old.astype(BF16)) * grow_wide + skip_wide[0:1, at] * x_float
        near = []
        for j in range(TILE // 128):
            h = (i * TILE + j * 128) // HEAD_DIM
            pair = x_in[:, j * 128 : (j + 1) * 128]
            near.append(
                mm(
                    jnp.concatenate([weights(h), weights(h + 1)], axis=1),
                    jnp.concatenate(
                        [jnp.where(first, pair, nothing), jnp.where(first, nothing, pair)], axis=0
                    ),
                )
            )
        y[:, at] = y_tile + jnp.concatenate(near, axis=1)
        state[:, at] = grow_wide[CHUNK - 1 :, :] * old + mm(b_t, (x_float * fade_wide).astype(BF16))


def local_part(s, x, b, c, dt, rate, skip, spread):
    length, feats = x.shape[1:]
    return pl.pallas_call(
        functools.partial(local_kernel, feats // HEAD_DIM),
        grid=(length // CHUNK,),
        in_specs=[
            pl.BlockSpec((1, CHUNK, feats), lambda i: (s, i, 0)),
            pl.BlockSpec((1, CHUNK, NSTATE), lambda i: (s, i, 0)),
            pl.BlockSpec((1, CHUNK, NSTATE), lambda i: (s, i, 0)),
            pl.BlockSpec((1, CHUNK, 128), lambda i: (s, i, 0)),
            pl.BlockSpec((1, 128), lambda i: (0, 0)),
            pl.BlockSpec((1, 128), lambda i: (0, 0)),
            pl.BlockSpec((128, feats), lambda i: (0, 0)),
        ],
        out_specs=pl.BlockSpec((CHUNK, feats), lambda i: (i, 0)),
        out_shape=jax.ShapeDtypeStruct((length, feats), F32),
        scratch_shapes=[pltpu.VMEM((NSTATE, feats), F32), pltpu.VMEM((8, feats), F32)],
        compiler_params=pltpu.CompilerParams(vmem_limit_bytes=24 << 20),
        cost_estimate=pl.CostEstimate(flops=6_000_000_000, bytes_accessed=9_000_000, transcendentals=0),
        name="local_part",
    )(x, b, c, dt, rate, skip, spread)


def gate_kernel(s, groups, heads, slots, me, *refs):
    pieces = refs[:groups]
    y, z, c, cum, gain, slot_pos, spread = refs[groups : groups + 7]
    rest = refs[groups + 7 :]
    carried = rest[:groups] if s else ()
    rest = rest[len(carried) :]
    gated, squares = rest[:2]
    sends = rest[2 : 2 + groups]
    entering, scaled, routed = rest[2 + groups :]
    step = pl.program_id(0)
    feats = spread.shape[1]
    rows = NSTATE // groups
    share = slots // groups

    @pl.when(step == 0)
    def _():
        for d in range(groups):
            entering[pl.ds(pl.multiple_of((me[0] ^ d) * rows, 8), rows), :] = pieces[d][...].astype(F32)

    grow = lane_parts(jnp.exp2(cum[...]), heads)
    c_out = c[0]
    square = jnp.zeros((CHUNK, 128), F32)
    for i in range(feats // TILE):
        at = pl.ds(i * TILE, TILE)
        far = mm(c_out, entering[:, at].astype(BF16)) * mm(grow, spread[:, at])
        half = z[0, :, at].astype(F32) * 0.5
        value = (y[:, at] + far) * (half + half * jnp.tanh(half))
        gated[:, at] = value
        scaled[:, at] = (value * gain[:, at]).astype(BF16)
        power = value * value
        for j in range(TILE // 128):
            square = square + power[:, j * 128 : (j + 1) * 128]
    total = jnp.sum(square, axis=1, keepdims=True)
    wide = jnp.broadcast_to(total, (CHUNK, 128))
    squares[pl.ds(step, 1), :] = wide.T[0:1, :]
    hi, mid, lo = three(wide)
    lane = lax.broadcasted_iota(jnp.int32, (CHUNK, EXTRA), 1)
    extra = jnp.where(lane == 0, hi, jnp.where(lane == 1, mid, jnp.where(lane == 2, lo, 0.0)))
    scaled[:, pl.ds(feats, EXTRA)] = extra.astype(BF16)
    start = (s * pl.num_programs(0) + step) * CHUNK
    here = slot_pos[...] == start + lax.broadcasted_iota(jnp.int32, (slots, CHUNK), 1)
    picked = mm(here.astype(F32).astype(BF16), scaled[...])

    @pl.when(step == 0)
    def _():
        routed[...] = picked

    @pl.when(step > 0)
    def _():
        routed[...] += picked

    @pl.when(step == pl.num_programs(0) - 1)
    def _():
        for d in range(groups):
            part = routed[pl.ds(d * share, share), :]
            if s:
                part = part + carried[d][...].astype(F32)
            sends[d][...] = part.astype(BF16)


def gate(s, me, pieces, y, z, c, cum, gain, slot_pos, spread, carried):
    length, feats = y.shape
    groups = len(pieces)
    slots = slot_pos.shape[0]
    rows = pieces[0].shape[0]
    fixed = lambda shape: pl.BlockSpec(shape, lambda i, m: (0,) * len(shape))
    send = (slots // groups, feats + EXTRA)
    return pl.pallas_call(
        functools.partial(gate_kernel, s, groups, feats // HEAD_DIM, slots),
        grid_spec=pltpu.PrefetchScalarGridSpec(
            num_scalar_prefetch=1,
            grid=(length // CHUNK,),
            in_specs=[fixed((rows, feats))] * groups
            + [
                pl.BlockSpec((CHUNK, feats), lambda i, m: (i, 0)),
                pl.BlockSpec((1, CHUNK, feats), lambda i, m: (s, i, 0)),
                pl.BlockSpec((1, CHUNK, NSTATE), lambda i, m: (s, i, 0)),
                pl.BlockSpec((CHUNK, 128), lambda i, m: (i, 0)),
                fixed((1, feats)),
                fixed((slots, 1)),
                fixed((128, feats)),
            ]
            + [fixed(send)] * len(carried),
            out_specs=[pl.BlockSpec((CHUNK, feats), lambda i, m: (i, 0)), fixed((8, 128))]
            + [fixed(send)] * groups,
            scratch_shapes=[
                pltpu.VMEM((NSTATE, feats), F32),
                pltpu.VMEM((CHUNK, feats + EXTRA), BF16),
                pltpu.VMEM((slots, feats + EXTRA), F32),
            ],
        ),
        out_shape=[jax.ShapeDtypeStruct((length, feats), F32), jax.ShapeDtypeStruct((8, 128), F32)]
        + [jax.ShapeDtypeStruct(send, BF16)] * groups,
        compiler_params=pltpu.CompilerParams(vmem_limit_bytes=32 << 20),
        cost_estimate=pl.CostEstimate(flops=1_000_000_000, bytes_accessed=15_000_000, transcendentals=0),
        name="gate",
    )(me, *pieces, y, z, c, cum, gain, slot_pos, spread, *carried)


def scale_kernel(gated, mine, other, gain, *rest):
    out = rest[-1]
    step = pl.program_id(0)
    mean = (mine[pl.ds(step, 1), :] + other[pl.ds(step, 1), :]) / (HEAD_TOTAL * HEAD_DIM)
    inv = jnp.broadcast_to(lax.rsqrt(mean + norm_eps), (CHUNK, 128)).T
    for i in range(gated.shape[1] // 128):
        at = pl.ds(i * 128, 128)
        out[0, :, at] = (gated[:, at] * inv * gain[:, at]).astype(BF16)


def scale(s, count, gated, mine, other, gain, before):
    length, feats = gated.shape
    fixed = lambda shape: pl.BlockSpec(shape, lambda i: (0,) * len(shape))
    return pl.pallas_call(
        scale_kernel,
        grid=(length // CHUNK,),
        in_specs=[
            pl.BlockSpec((CHUNK, feats), lambda i: (i, 0)),
            fixed((8, 128)),
            fixed((8, 128)),
            fixed((1, feats)),
        ]
        + [pl.BlockSpec(memory_space=pl.ANY)] * len(before),
        out_specs=pl.BlockSpec((1, CHUNK, feats), lambda i: (s, i, 0)),
        out_shape=jax.ShapeDtypeStruct((count, length, feats), BF16),
        input_output_aliases={4: 0} if before else {},
        compiler_params=pltpu.CompilerParams(vmem_limit_bytes=24 << 20),
        cost_estimate=pl.CostEstimate(flops=10_000_000, bytes_accessed=8_000_000, transcendentals=0),
        name="scale",
    )(gated, mine, other, gain, *before)


def expert_kernel(count, core, *refs):
    own, other = refs[:count], refs[count : 2 * count]
    w1, b1, w2 = refs[2 * count : 2 * count + 3]
    outs = refs[2 * count + 3 : 3 * count + 3]
    rows_a, rows_b = refs[3 * count + 3 :]
    share, wide = own[0].shape
    feats = wide - EXTRA
    for k in range(count):
        at = pl.ds(k * share, share)
        rows_a[at, :] = own[k][...]
        rows_b[at, :] = other[k][...]
    sums = jnp.zeros((count * share, 1), F32)
    for ref in (rows_a, rows_b):
        part = ref[:, pl.ds(feats, EXTRA)].astype(F32)
        lane = lax.broadcasted_iota(jnp.int32, part.shape, 1)
        sums = sums + jnp.sum(jnp.where(lane < 3, part, 0.0), axis=1, keepdims=True)
    inv = lax.rsqrt(sums / (HEAD_TOTAL * HEAD_DIM) + norm_eps)
    lower = pl.ds(pl.multiple_of(core[0] * feats, 128), feats)
    upper = pl.ds(pl.multiple_of((1 - core[0]) * feats, 128), feats)
    pre = mm(rows_a[:, pl.ds(0, feats)], w1[0, lower, :]) + mm(
        rows_b[:, pl.ds(0, feats)], w1[0, upper, :]
    )
    pre = pre * inv + b1[...]
    hidden = jax.nn.gelu(pre).astype(BF16).astype(F32)
    value = jnp.sum(hidden * w2[...].astype(F32), axis=1, keepdims=True)
    value = jnp.broadcast_to(value, (count * share, 128))
    for k in range(count):
        outs[k][...] = value[k * share : (k + 1) * share]


def expert(core, own, other, w1, b1, w2):
    count = len(own)
    share, wide = own[0].shape
    vmem = pl.BlockSpec(memory_space=pltpu.VMEM)
    return pl.pallas_call(
        functools.partial(expert_kernel, count),
        in_specs=[pl.BlockSpec(memory_space=pltpu.SMEM)] + [vmem] * (2 * count + 3),
        out_specs=[vmem] * count,
        out_shape=[jax.ShapeDtypeStruct((share, 128), F32)] * count,
        scratch_shapes=[pltpu.VMEM((count * share, wide), BF16)] * 2,
        compiler_params=pltpu.CompilerParams(vmem_limit_bytes=24 << 20),
        cost_estimate=pl.CostEstimate(flops=400_000_000, bytes_accessed=6_000_000, transcendentals=0),
        name="expert",
    )(core, *own, *other, w1, b1, w2)


def body(
    x_inner,
    z_gate,
    b_input,
    c_output,
    step_sizes,
    decay_log,
    skip_gain,
    norm_gain,
    goal_pos,
    goal_owner,
    value_w1,
    value_b1,
    value_w2,
):
    count, length, feats = x_inner.shape
    heads = step_sizes.shape[2]
    devices = lax.axis_size("seq")
    planes = PLANES
    groups = devices // planes
    index = lax.axis_index("seq")
    place, plane = index % groups, index // groups
    me = place.reshape(1).astype(jnp.int32)
    core = lax.axis_index("head").reshape(1).astype(jnp.int32)

    def permute(value, where):
        return lax.ppermute(value, "seq", where)

    def across(value, d):
        return permute(value, [(i, i ^ d) for i in range(devices)])

    def swap(value):
        return lax.ppermute(value, "head", [(0, 1), (1, 0)])

    def triple(v, fill):
        return jnp.concatenate(
            [v, v, v, jnp.full(v.shape[:-1] + (128 - 3 * heads,), fill, F32)], axis=-1
        )

    lanes = np.arange(128)
    spread = jnp.asarray(
        (lanes[:, None] % heads == np.arange(feats)[None, :] // HEAD_DIM)
        & (lanes[:, None] < 3 * heads),
        BF16,
    )
    dt = triple(step_sizes, 1.0)
    rate = triple(-jnp.exp(decay_log) * LOG2E, 0.0)[None]
    skip = triple(skip_gain, 0.0)[None]
    gain = norm_gain[None]

    goal_dev = goal_pos.shape[1]
    owners = goal_owner.reshape(-1)
    positions = (
        goal_pos - index * length + length * jnp.arange(count, dtype=jnp.int32)[:, None]
    ).reshape(-1)
    ids = jnp.arange(owners.shape[0])
    same = (owners[:, None] == owners[None, :]) & (ids[None, :] < ids[:, None])
    rank = jnp.sum(same.astype(jnp.int32), axis=1)
    slot = (((owners % groups) ^ place) * planes + ((owners // groups) ^ plane)) * CAP + rank
    slots = devices * CAP
    taken = jnp.arange(slots)[:, None] == slot[None, :]
    slot_pos = jnp.max(jnp.where(taken, positions[None, :], -1), axis=1, keepdims=True)

    summaries = [
        summary(s, me, x_inner, b_input, dt, rate, spread, groups) for s in range(count)
    ]
    locals_ = [
        local_part(s, x_inner, b_input, c_output, dt, rate, skip, spread) for s in range(count)
    ]
    gathered = [
        [own[0]] + [across(own[d], d) for d in range(1, groups)] for own in summaries
    ]
    totals = [plane_total(me, spread, pieces) for pieces in gathered]
    below = [
        [
            permute(total, [(i, i + k * groups) for i in range(devices - k * groups)])
            for k in range(1, planes)
        ]
        for total in totals
    ]
    incoming = [incoming_states(me, spread, p, t) for p, t in zip(gathered, below)]
    entering = [[own[0]] + [across(own[d], d) for d in range(1, groups)] for own in incoming]

    gated, mine, sends = [], [], ()
    for s in range(count):
        made = gate(
            s,
            me,
            entering[s],
            locals_[s],
            z_gate,
            c_output,
            summaries[s][-1],
            gain,
            slot_pos,
            spread,
            sends,
        )
        gated.append(made[0])
        mine.append(made[1])
        sends = tuple(made[2:])
    others = [swap(v) for v in mine]
    layer_out = ()
    for s in range(count):
        layer_out = (scale(s, count, gated[s], mine[s], others[s], gain, layer_out),)

    near = [sends[0]] + [across(sends[d], d) for d in range(1, groups)]
    far = [
        jnp.concatenate([v[k * CAP : (k + 1) * CAP] for v in near], axis=0) for k in range(planes)
    ]
    own = [far[0]] + [across(far[k], k * groups) for k in range(1, planes)]
    other = [swap(v) for v in own]
    answers = expert(core, own, other, value_w1, value_b1, value_w2)
    answers = [v[:, :1] for v in answers]
    back = [answers[0]] + [across(answers[k], k * groups) for k in range(1, planes)]
    table = jnp.concatenate(back, axis=1)
    table = table + swap(table)
    tables = [table] + [across(table, d) for d in range(1, groups)]
    flat = jnp.concatenate(
        [t[d * CAP : (d + 1) * CAP].T.reshape(-1) for d, t in enumerate(tables)]
    )
    values = jnp.sum(jnp.where(taken, flat[:, None], 0.0), axis=0).reshape(count, goal_dev)
    return (layer_out[0], values)


def solution(mesh):
    placed = (
        P(None, "seq", "head"),
        P(None, "seq", "head"),
        P(None, "seq", None),
        P(None, "seq", None),
        P(None, "seq", "head"),
        P("head"),
        P("head"),
        P("head"),
        P(None, "seq"),
        P(None, "seq"),
        P("seq", None, "head"),
        P("seq", "head"),
        P("seq", "head"),
    )
    return jax.shard_map(
        body,
        mesh=mesh,
        in_specs=placed,
        out_specs=(P(None, "seq", "head"), P(None, "seq")),
        check_vma=False,
    )
```

```python
import functools

import jax
import jax.numpy as jnp
import numpy as np
from jax import lax
from jax.experimental import pallas as pl
from jax.experimental.pallas import tpu as pltpu
from jax.sharding import PartitionSpec as P

HEAD_TOTAL = 80
HEAD_DIM = 64
NSTATE = 128
CAP = 4
PLANES = 4
CHUNK = 128
TILE = 256
EXTRA = 128
LOG2E = 1.4426950408889634
norm_eps = 1e-05
F32 = jnp.float32
BF16 = jnp.bfloat16
HIGHEST = lax.Precision.HIGHEST


def mm(a, b):
    return jnp.dot(a, b, preferred_element_type=F32)


def lane_parts(v, heads):
    hi = v.astype(BF16)
    rest = v - hi.astype(F32)
    mid = rest.astype(BF16)
    lo = (rest - mid.astype(F32)).astype(BF16)
    lane = lax.broadcasted_iota(jnp.int32, v.shape, 1)
    return jnp.where(
        lane < heads, hi.astype(F32), jnp.where(lane < 2 * heads, mid.astype(F32), lo.astype(F32))
    ).astype(BF16)


def three(v):
    hi = v.astype(BF16).astype(F32)
    mid = (v - hi).astype(BF16).astype(F32)
    return hi, mid, v - hi - mid


def step_chunk(dt, k):
    part = dt[0, :, pl.ds(k * CHUNK, CHUNK)]
    fill = jnp.ones((128 - 3 * part.shape[0], CHUNK), F32)
    return jnp.concatenate([part, part, part, fill], axis=0).T


def total_rows(total, rows):
    hi, mid, lo = three(total)
    row = lax.broadcasted_iota(jnp.int32, (rows, EXTRA), 0)
    return jnp.where(
        row == 0, hi, jnp.where(row == 1, mid, jnp.where(row == 2, lo, 0.0))
    ).astype(BF16)


def tri_mask():
    rows = lax.broadcasted_iota(jnp.int32, (CHUNK, CHUNK), 0)
    cols = lax.broadcasted_iota(jnp.int32, (CHUNK, CHUNK), 1)
    return rows >= cols


def summary_kernel(groups, heads, me, x, b, dt, rate, spread, *rest):
    outs, (cum, parts, bt, st) = rest[:groups], rest[groups:]
    s, step = pl.program_id(0), pl.program_id(1)
    length = dt.shape[2]
    width = x.shape[2]
    rows = NSTATE // groups
    mine = pl.ds(pl.multiple_of(s * rows, rows), rows)

    @pl.when(step == 0)
    def _():
        tri = tri_mask().astype(F32)
        steps = [step_chunk(dt, k) for k in range(length // CHUNK)]
        before = jnp.zeros((1, 128), F32)
        for k in range(length // CHUNK):
            at = pl.ds(k * CHUNK, CHUNK)
            part = (
                jnp.dot(tri, steps[k] * rate[...], precision=HIGHEST, preferred_element_type=F32)
                + before
            )
            cum[0, at, :] = part
            before = part[CHUNK - 1 :, :]
            bt[:, at] = b[0, at, :].astype(F32).T.astype(BF16)
        for k in range(length // CHUNK):
            at = pl.ds(k * CHUNK, CHUNK)
            parts[at, :] = lane_parts(jnp.exp2(before - cum[0, at, :]) * steps[k], heads)
        extra = total_rows(before, rows)
        for d in range(groups):
            outs[d][mine, pl.ds(outs[d].shape[1] - EXTRA, EXTRA)] = extra

    for i in range(width // TILE):
        at = pl.ds(i * TILE, TILE)
        wide = spread[:, pl.ds(pl.multiple_of(step * width + i * TILE, TILE), TILE)]
        weighted = (x[0, :, at].astype(F32) * mm(parts[...], wide)).astype(BF16)
        st[:, at] = mm(bt[...], weighted)
    for d in range(groups):
        outs[d][mine, pl.ds(pl.multiple_of(step * width, 128), width)] = st[
            pl.ds(pl.multiple_of((me[0] ^ d) * rows, 8), rows), :
        ].astype(BF16)


def summary(me, x, b, dt, rate, spread, groups):
    count, length, feats = x.shape
    width = 512
    heads = feats // HEAD_DIM
    piece = (count * NSTATE // groups, feats + EXTRA)
    return pl.pallas_call(
        functools.partial(summary_kernel, groups, heads),
        grid_spec=pltpu.PrefetchScalarGridSpec(
            num_scalar_prefetch=1,
            grid=(count, feats // width),
            in_specs=[
                pl.BlockSpec((1, length, width), lambda s, i, m: (s, 0, i)),
                pl.BlockSpec((1, length, NSTATE), lambda s, i, m: (s, 0, 0)),
                pl.BlockSpec((1, heads, length), lambda s, i, m: (s, 0, 0)),
                pl.BlockSpec((1, 128), lambda s, i, m: (0, 0)),
                pl.BlockSpec(memory_space=pltpu.VMEM),
            ],
            out_specs=[pl.BlockSpec(piece, lambda s, i, m: (0, 0))] * groups
            + [pl.BlockSpec((1, length, 128), lambda s, i, m: (s, 0, 0))],
            scratch_shapes=[
                pltpu.VMEM((length, 128), BF16),
                pltpu.VMEM((NSTATE, length), BF16),
                pltpu.VMEM((NSTATE, width), F32),
            ],
        ),
        out_shape=[jax.ShapeDtypeStruct(piece, BF16)] * groups
        + [jax.ShapeDtypeStruct((count, length, 128), F32)],
        compiler_params=pltpu.CompilerParams(vmem_limit_bytes=60 << 20),
        cost_estimate=pl.CostEstimate(flops=2_800_000_000, bytes_accessed=8_000_000, transcendentals=0),
        name="summary",
    )(me, x, b, dt, rate, spread)


def totals_of(views, feats):
    out = []
    for view in views:
        block = view[0:8, pl.ds(feats, EXTRA)].astype(F32)
        out.append(block[0:1] + block[1:2] + block[2:3])
    return out


def factors(totals, spread, heads, tile):
    fill = [jnp.zeros((1, 128), F32)] * (-len(totals) % 16)
    stacked = jnp.concatenate(totals + fill, axis=0)
    return mm(lane_parts(jnp.exp2(stacked), heads), spread[:, tile])


def plane_kernel(groups, heads, count, me, spread, *rest):
    pieces, (out, ordered) = rest[:groups], rest[-2:]
    feats = spread.shape[1]
    rows = out.shape[0] // count
    for d in range(groups):
        ordered[d] = pieces[d][...].astype(F32)
    for s in range(count):
        at_rows = pl.ds(s * rows, rows)
        views = [ordered.at[me[0] ^ p, at_rows, :] for p in range(groups)]
        totals = totals_of(views, feats)
        for i in range(feats // TILE):
            at = pl.ds(i * TILE, TILE)
            decay = factors(totals, spread, heads, at)
            total = views[0][:, at]
            for p in range(1, groups):
                total = decay[p : p + 1] * total + views[p][:, at]
            out[at_rows, at] = total.astype(BF16)
        out[at_rows, pl.ds(feats, EXTRA)] = total_rows(
            functools.reduce(lambda a, b: a + b, totals), rows
        )


def plane_total(me, spread, pieces, count, after):
    groups = len(pieces)
    rows, wide = pieces[0].shape
    heads = spread.shape[1] // HEAD_DIM
    vmem = pl.BlockSpec(memory_space=pltpu.VMEM)
    return pl.pallas_call(
        functools.partial(plane_kernel, groups, heads, count),
        in_specs=[pl.BlockSpec(memory_space=pltpu.SMEM)]
        + [vmem] * (groups + 1)
        + [pl.BlockSpec(memory_space=pl.ANY)] * len(after),
        out_specs=vmem,
        out_shape=jax.ShapeDtypeStruct((rows, wide), BF16),
        scratch_shapes=[pltpu.VMEM((groups, rows, wide), F32)],
        compiler_params=pltpu.CompilerParams(vmem_limit_bytes=12 << 20),
        cost_estimate=pl.CostEstimate(flops=10_000_000, bytes_accessed=1_500_000, transcendentals=0),
        name="plane_total",
    )(me, spread, *pieces, *after)


def incoming_kernel(groups, hops, heads, count, me, spread, *rest):
    pieces, below = rest[:groups], rest[groups : groups + hops]
    outs = rest[-groups - 2 : -2]
    ordered, results = rest[-2:]
    feats = spread.shape[1]
    rows = outs[0].shape[0] // count
    for d in range(groups):
        ordered[d] = pieces[d][...].astype(F32)
    for s in range(count):
        at_rows = pl.ds(s * rows, rows)
        views = [ordered.at[me[0] ^ p, at_rows, :] for p in range(groups)]
        under = [ref.at[at_rows, :] for ref in below]
        totals = totals_of(views, feats) + totals_of(under, feats)
        for i in range(feats // TILE):
            at = pl.ds(i * TILE, TILE)
            decay = factors(totals, spread, heads, at)
            state = jnp.zeros((rows, TILE), F32)
            for k in range(hops - 1, -1, -1):
                state = decay[groups + k : groups + k + 1] * state + under[k][:, at].astype(F32)
            for p in range(groups):
                results[me[0] ^ p, at_rows, at] = state
                if p < groups - 1:
                    state = decay[p : p + 1] * state + views[p][:, at]
    for d in range(groups):
        outs[d][...] = results[d].astype(BF16)


def incoming_states(me, spread, pieces, below, count, after):
    groups, hops = len(pieces), len(below)
    rows, wide = pieces[0].shape
    feats = spread.shape[1]
    vmem = pl.BlockSpec(memory_space=pltpu.VMEM)
    return pl.pallas_call(
        functools.partial(incoming_kernel, groups, hops, feats // HEAD_DIM, count),
        in_specs=[pl.BlockSpec(memory_space=pltpu.SMEM)]
        + [vmem] * (1 + groups + hops)
        + [pl.BlockSpec(memory_space=pl.ANY)] * len(after),
        out_specs=[vmem] * groups,
        out_shape=[jax.ShapeDtypeStruct((rows, feats), BF16)] * groups,
        scratch_shapes=[
            pltpu.VMEM((groups, rows, wide), F32),
            pltpu.VMEM((groups, rows, feats), F32),
        ],
        compiler_params=pltpu.CompilerParams(vmem_limit_bytes=14 << 20),
        cost_estimate=pl.CostEstimate(flops=10_000_000, bytes_accessed=2_500_000, transcendentals=0),
        name="incoming_states",
    )(me, spread, *pieces, *below, *after)


def local_kernel(heads, first_head, x, b, c, dt, rate, skip, spread, *rest):
    y, token, state, skip_wide = rest[-4:]
    step = pl.program_id(0)
    feats = x.shape[2]
    offset = first_head * HEAD_DIM

    @pl.when(step == 0)
    def _():
        state[...] = jnp.zeros_like(state)
        token[...] = jnp.zeros_like(token)
        for i in range(feats // TILE):
            at = pl.ds(i * TILE, TILE)
            skip_wide[:, at] = mm(
                lane_parts(jnp.broadcast_to(skip[...], (16, 128)), heads),
                spread[:, pl.ds(offset + i * TILE, TILE)],
            )[:8]

    keep = tri_mask()
    steps = step_chunk(dt, 0)
    cum = jnp.dot(
        keep.astype(F32), steps * rate[...], precision=HIGHEST, preferred_element_type=F32
    )
    from_row = (cum - jnp.log2(steps)).T
    b_in, c_out = b[0], c[0]
    scores = lax.dot_general(c_out, b_in, (((1,), (1,)), ((), ())), preferred_element_type=F32)
    b_t = b_in.astype(F32).T.astype(BF16)
    grow = lane_parts(jnp.exp2(cum), heads)
    fade = lane_parts(jnp.exp2(cum[CHUNK - 1 :, :] - cum) * steps, heads)
    first = lax.broadcasted_iota(jnp.int32, (CHUNK, 128), 1) < HEAD_DIM
    nothing = jnp.zeros((CHUNK, 128), BF16)

    def weights(h):
        return jnp.where(
            keep, scores * jnp.exp2(cum[:, h : h + 1] - from_row[h : h + 1, :]), 0.0
        ).astype(BF16)

    for i in range(feats // TILE):
        at = pl.ds(i * TILE, TILE)
        wide = spread[:, pl.ds(offset + i * TILE, TILE)]
        grow_wide = mm(grow, wide)
        fade_wide = mm(fade, wide)
        x_in = x[0, :, at]
        x_float = x_in.astype(F32)
        old = state[:, at]
        y_tile = mm(c_out, old.astype(BF16)) * grow_wide + skip_wide[0:1, at] * x_float
        near = []
        for j in range(TILE // 128):
            h = first_head + (i * TILE + j * 128) // HEAD_DIM
            pair = x_in[:, j * 128 : (j + 1) * 128]
            near.append(
                mm(
                    jnp.concatenate([weights(h), weights(h + 1)], axis=1),
                    jnp.concatenate(
                        [jnp.where(first, pair, nothing), jnp.where(first, nothing, pair)], axis=0
                    ),
                )
            )
        y[0, :, at] = (y_tile + jnp.concatenate(near, axis=1)).astype(BF16)
        state[:, at] = grow_wide[CHUNK - 1 :, :] * old + mm(b_t, (x_float * fade_wide).astype(BF16))


def local_part(s, part, parts, x, b, c, dt, rate, skip, spread, before, after):
    count, length, feats = x.shape[0], x.shape[1], x.shape[2] // parts
    heads = x.shape[2] // HEAD_DIM
    return pl.pallas_call(
        functools.partial(local_kernel, heads, part * feats // HEAD_DIM),
        grid=(length // CHUNK,),
        in_specs=[
            pl.BlockSpec((1, CHUNK, feats), lambda i: (s, i, part)),
            pl.BlockSpec((1, CHUNK, NSTATE), lambda i: (s, i, 0)),
            pl.BlockSpec((1, CHUNK, NSTATE), lambda i: (s, i, 0)),
            pl.BlockSpec((1, heads, CHUNK), lambda i: (s, 0, i)),
            pl.BlockSpec((1, 128), lambda i: (0, 0)),
            pl.BlockSpec((1, 128), lambda i: (0, 0)),
            pl.BlockSpec(memory_space=pltpu.VMEM),
        ]
        + [pl.BlockSpec(memory_space=pl.ANY)] * (len(before) + len(after)),
        out_specs=[
            pl.BlockSpec((1, CHUNK, feats), lambda i: (s, i, part)),
            pl.BlockSpec((8, 128), lambda i: (0, 0)),
        ],
        out_shape=[
            jax.ShapeDtypeStruct((count, length, feats * parts), BF16),
            jax.ShapeDtypeStruct((8, 128), F32),
        ],
        input_output_aliases={7: 0} if before else {},
        scratch_shapes=[pltpu.VMEM((NSTATE, feats), F32), pltpu.VMEM((8, feats), F32)],
        compiler_params=pltpu.CompilerParams(vmem_limit_bytes=60 << 20),
        cost_estimate=pl.CostEstimate(flops=6_000_000_000, bytes_accessed=9_000_000, transcendentals=0),
        name="local_part",
    )(x, b, c, dt, rate, skip, spread, *before, *after)


def gate_kernel(groups, heads, slots, me, *refs):
    pieces, refs = refs[:groups], refs[groups:]
    y, z, c, cum, gain, slot_pos, spread = refs[:7]
    gated, squares = refs[7:9]
    sends = refs[9 : 9 + groups]
    entering, routed = refs[9 + groups :]
    s, step = pl.program_id(0), pl.program_id(1)
    feats = spread.shape[1]
    rows = NSTATE // groups
    share = slots // groups
    row = s * pl.num_programs(1) + step

    @pl.when(step == 0)
    def _():
        mine = pl.ds(pl.multiple_of(s * rows, 8), rows)
        for d in range(groups):
            entering[pl.ds(pl.multiple_of((me[0] ^ d) * rows, 8), rows), :] = pieces[d][
                mine, :
            ].astype(F32)

    @pl.when(row == 0)
    def _():
        routed[...] = jnp.zeros_like(routed)

    grow = lane_parts(jnp.exp2(cum[0]), heads)
    c_out = c[0]
    square = jnp.zeros((CHUNK, 128), F32)
    here = slot_pos[...] == row * CHUNK + lax.broadcasted_iota(jnp.int32, (slots, CHUNK), 1)
    pick = here.astype(F32).astype(BF16)
    for i in range(feats // TILE):
        at = pl.ds(i * TILE, TILE)
        far = mm(c_out, entering[:, at].astype(BF16)) * mm(grow, spread[:, at])
        half = z[0, :, at].astype(F32) * 0.5
        value = (y[0, :, at].astype(F32) + far) * (half + half * jnp.tanh(half))
        kept = (value * gain[:, at]).astype(BF16)
        gated[0, :, at] = kept
        power = value * value
        for j in range(TILE // 128):
            square = square + power[:, j * 128 : (j + 1) * 128]
    wide = jnp.broadcast_to(jnp.sum(square, axis=1, keepdims=True), (CHUNK, 128))
    squares[pl.ds(row, 1), :] = wide.T[0:1, :]
    hi, mid, lo = three(wide)
    lane = lax.broadcasted_iota(jnp.int32, (CHUNK, EXTRA), 1)
    extra = jnp.where(lane == 0, hi, jnp.where(lane == 1, mid, jnp.where(lane == 2, lo, 0.0)))
    routed[:, pl.ds(0, feats)] += mm(pick, gated[0])
    routed[:, pl.ds(feats, EXTRA)] += mm(pick, extra.astype(BF16))

    @pl.when(row == pl.num_programs(0) * pl.num_programs(1) - 1)
    def _():
        for d in range(groups):
            sends[d][...] = routed[pl.ds(d * share, share), :].astype(BF16)


def gate(me, pieces, y, z, c, cum, gain, slot_pos, spread):
    count, length, feats = z.shape
    groups = len(pieces)
    slots = slot_pos.shape[0]
    fixed = lambda shape: pl.BlockSpec(shape, lambda s, i, m: (0,) * len(shape))
    block = lambda width: pl.BlockSpec((1, CHUNK, width), lambda s, i, m: (s, i, 0))
    send = (slots // groups, feats + EXTRA)
    lines = (count * length // CHUNK, 128)
    return pl.pallas_call(
        functools.partial(gate_kernel, groups, feats // HEAD_DIM, slots),
        grid_spec=pltpu.PrefetchScalarGridSpec(
            num_scalar_prefetch=1,
            grid=(count, length // CHUNK),
            in_specs=[fixed(pieces[0].shape)] * groups
            + [block(feats), block(feats), block(NSTATE), block(128)]
            + [fixed((1, feats)), fixed((slots, 1)), pl.BlockSpec(memory_space=pltpu.VMEM)],
            out_specs=[block(feats), fixed(lines)] + [fixed(send)] * groups,
            scratch_shapes=[
                pltpu.VMEM((NSTATE, feats), F32),
                pltpu.VMEM((slots, feats + EXTRA), F32),
            ],
        ),
        out_shape=[jax.ShapeDtypeStruct((count, length, feats), BF16), jax.ShapeDtypeStruct(lines, F32)]
        + [jax.ShapeDtypeStruct(send, BF16)] * groups,
        compiler_params=pltpu.CompilerParams(vmem_limit_bytes=60 << 20),
        cost_estimate=pl.CostEstimate(flops=2_000_000_000, bytes_accessed=20_000_000, transcendentals=0),
        name="gate",
    )(me, *pieces, y, z, c, cum, gain, slot_pos, spread)


def scale_kernel(gated, mine, other, *rest):
    out, token = rest[-2:]
    token[...] = jnp.zeros_like(token)
    row = pl.ds(pl.program_id(0) * pl.num_programs(1) + pl.program_id(1), 1)
    mean = (mine[row, :] + other[row, :]) / (HEAD_TOTAL * HEAD_DIM)
    inv = jnp.broadcast_to(lax.rsqrt(mean + norm_eps), (CHUNK, 128)).T
    for i in range(gated.shape[2] // 128):
        at = pl.ds(i * 128, 128)
        out[0, :, at] = (gated[0, :, at].astype(F32) * inv).astype(BF16)


def scale(gated, mine, other, after):
    count, length, feats = gated.shape
    fixed = lambda shape: pl.BlockSpec(shape, lambda s, i: (0,) * len(shape))
    block = pl.BlockSpec((1, CHUNK, feats), lambda s, i: (s, i, 0))
    return pl.pallas_call(
        scale_kernel,
        grid=(count, length // CHUNK),
        in_specs=[block, fixed(mine.shape), fixed(mine.shape)]
        + [pl.BlockSpec(memory_space=pl.ANY)] * len(after),
        out_specs=[block, fixed((8, 128))],
        out_shape=[jax.ShapeDtypeStruct(gated.shape, BF16), jax.ShapeDtypeStruct((8, 128), F32)],
        compiler_params=pltpu.CompilerParams(vmem_limit_bytes=10 << 20),
        cost_estimate=pl.CostEstimate(flops=10_000_000, bytes_accessed=8_000_000, transcendentals=0),
        name="scale",
    )(gated, mine, other, *after)


def join_kernel(count, *refs):
    out = refs[-1]
    share = refs[0].shape[0]
    for k in range(count):
        out[pl.ds(k * share, share), :] = refs[k][...]


def join(parts, after):
    share, wide = parts[0].shape
    vmem = pl.BlockSpec(memory_space=pltpu.VMEM)
    return pl.pallas_call(
        functools.partial(join_kernel, len(parts)),
        in_specs=[vmem] * len(parts) + [pl.BlockSpec(memory_space=pl.ANY)] * len(after),
        out_specs=vmem,
        out_shape=jax.ShapeDtypeStruct((len(parts) * share, wide), BF16),
        compiler_params=pltpu.CompilerParams(vmem_limit_bytes=10 << 20),
        cost_estimate=pl.CostEstimate(flops=1_000_000, bytes_accessed=700_000, transcendentals=0),
        name="join",
    )(*parts, *after)


def expert_kernel(core, own, other, w1, b1, w2, *outs):
    feats = own.shape[1] - EXTRA
    share = outs[0].shape[0]
    sums = jnp.zeros((own.shape[0], 1), F32)
    for ref in (own, other):
        part = ref[:, pl.ds(feats, EXTRA)].astype(F32)
        lane = lax.broadcasted_iota(jnp.int32, part.shape, 1)
        sums = sums + jnp.sum(jnp.where(lane < 3, part, 0.0), axis=1, keepdims=True)
    inv = lax.rsqrt(sums / (HEAD_TOTAL * HEAD_DIM) + norm_eps)
    lower = pl.ds(pl.multiple_of(core[0] * feats, 128), feats)
    upper = pl.ds(pl.multiple_of((1 - core[0]) * feats, 128), feats)
    pre = mm(own[:, pl.ds(0, feats)], w1[0, lower, :]) + mm(
        other[:, pl.ds(0, feats)], w1[0, upper, :]
    )
    pre = pre * inv + b1[...]
    hidden = jax.nn.gelu(pre).astype(BF16).astype(F32)
    value = jnp.sum(hidden * w2[...].astype(F32), axis=1, keepdims=True)
    value = jnp.broadcast_to(value, (own.shape[0], 128))
    for k, out in enumerate(outs):
        out[...] = value[k * share : (k + 1) * share]


def expert(core, own, other, w1, b1, w2, count):
    share = own.shape[0] // count
    vmem = pl.BlockSpec(memory_space=pltpu.VMEM)
    return pl.pallas_call(
        expert_kernel,
        in_specs=[pl.BlockSpec(memory_space=pltpu.SMEM)] + [vmem] * 5,
        out_specs=[vmem] * count,
        out_shape=[jax.ShapeDtypeStruct((share, 128), F32)] * count,
        compiler_params=pltpu.CompilerParams(vmem_limit_bytes=14 << 20),
        cost_estimate=pl.CostEstimate(flops=400_000_000, bytes_accessed=6_000_000, transcendentals=0),
        name="expert",
    )(core, own, other, w1, b1, w2)


def body(
    x_inner,
    z_gate,
    b_input,
    c_output,
    step_sizes,
    decay_log,
    skip_gain,
    norm_gain,
    goal_pos,
    goal_owner,
    value_w1,
    value_b1,
    value_w2,
):
    count, length, feats = x_inner.shape
    heads = step_sizes.shape[2]
    devices = lax.axis_size("seq")
    planes = PLANES
    groups = devices // planes
    index = lax.axis_index("seq")
    place, plane = index % groups, index // groups
    me = place.reshape(1).astype(jnp.int32)
    core = lax.axis_index("head").reshape(1).astype(jnp.int32)

    def permute(value, where):
        return lax.ppermute(value, "seq", where)

    def across(value, d):
        return permute(value, [(i, i ^ d) for i in range(devices)])

    def swap(value):
        return lax.ppermute(value, "head", [(0, 1), (1, 0)])

    def triple(v, fill):
        return jnp.concatenate(
            [v, v, v, jnp.full(v.shape[:-1] + (128 - 3 * heads,), fill, F32)], axis=-1
        )

    lanes = np.arange(128)
    spread = jnp.asarray(
        (lanes[:, None] % heads == np.arange(feats)[None, :] // HEAD_DIM)
        & (lanes[:, None] < 3 * heads),
        BF16,
    )
    dt = jnp.swapaxes(step_sizes, 1, 2)
    rate = triple(-jnp.exp(decay_log) * LOG2E, 0.0)[None]
    skip = triple(skip_gain, 0.0)[None]
    gain = norm_gain[None]

    goal_dev = goal_pos.shape[1]
    owners = goal_owner.reshape(-1)
    positions = (
        goal_pos - index * length + length * jnp.arange(count, dtype=jnp.int32)[:, None]
    ).reshape(-1)
    ids = jnp.arange(owners.shape[0])
    same = (owners[:, None] == owners[None, :]) & (ids[None, :] < ids[:, None])
    rank = jnp.sum(same.astype(jnp.int32), axis=1)
    slot = (((owners % groups) ^ place) * planes + ((owners // groups) ^ plane)) * CAP + rank
    slots = devices * CAP
    taken = jnp.arange(slots)[:, None] == slot[None, :]
    slot_pos = jnp.max(jnp.where(taken, positions[None, :], -1), axis=1, keepdims=True)

    nothing = jnp.zeros((1,), jnp.int32)

    def upward(value, hops):
        hop = hops * groups
        return permute(value, [(i, i + hop) for i in range(devices - hop)])

    def local(s, part, parts, before, after):
        return local_part(
            s, part, parts, x_inner, b_input, c_output, dt, rate, skip, spread, before, after
        )

    def spread_out(own):
        return [own[0]] + [across(own[d], d) for d in range(1, groups)]

    *own, cum = summary(me, x_inner, b_input, dt, rate, spread, groups)
    gathered = spread_out(own)
    y, token = local(0, 0, 1, (), (own[0],))
    total = plane_total(me, spread, gathered, count, (token,))
    one = upward(total, 1)
    y, token = local(1, 0, 2, (y,), (total,))
    pair = plane_total(nothing, spread, [one, total], count, (token,))
    two = upward(pair, 2)
    y, token = local(1, 1, 2, (y,), (pair,))
    entering = spread_out(incoming_states(me, spread, gathered, [one, two], count, (token,)))
    gated, mine, *sends = gate(
        me, entering, y, z_gate, c_output, cum, gain, slot_pos, spread
    )
    near = spread_out(sends)
    far = [
        jnp.concatenate([v[k * CAP : (k + 1) * CAP] for v in near], axis=0) for k in range(planes)
    ]
    own = [far[0]] + [across(far[k], k * groups) for k in range(1, planes)]
    layer_out, token = scale(gated, mine, swap(mine), (far[1],))
    rows = join(own, (token,))
    answers = expert(core, rows, swap(rows), value_w1, value_b1, value_w2, planes)
    answers = [v[:, :1] for v in answers]
    back = [answers[0]] + [across(answers[k], k * groups) for k in range(1, planes)]
    table = jnp.concatenate(back, axis=1)
    table = table + swap(table)
    tables = [table] + [across(table, d) for d in range(1, groups)]
    flat = jnp.concatenate(
        [t[d * CAP : (d + 1) * CAP].T.reshape(-1) for d, t in enumerate(tables)]
    )
    values = jnp.sum(jnp.where(taken, flat[:, None], 0.0), axis=0).reshape(count, goal_dev)
    return (layer_out, values)


def solution(mesh):
    placed = (
        P(None, "seq", "head"),
        P(None, "seq", "head"),
        P(None, "seq", None),
        P(None, "seq", None),
        P(None, "seq", "head"),
        P("head"),
        P("head"),
        P("head"),
        P(None, "seq"),
        P(None, "seq"),
        P("seq", None, "head"),
        P("seq", "head"),
        P("seq", "head"),
    )
    return jax.shard_map(
        body,
        mesh=mesh,
        in_specs=placed,
        out_specs=(P(None, "seq", "head"), P(None, "seq")),
        check_vma=False,
    )
```

```python
import functools

import jax
import jax.numpy as jnp
import numpy as np
from jax import lax
from jax.experimental import pallas as pl
from jax.experimental.pallas import tpu as pltpu
from jax.sharding import PartitionSpec as P

HEAD_TOTAL = 80
HEAD_DIM = 64
NSTATE = 128
CAP = 4
PLANES = 4
CHUNK = 128
GATE_ROWS = 256
TILE = 256
EXTRA = 128
LOG2E = 1.4426950408889634
norm_eps = 1e-05
F32 = jnp.float32
BF16 = jnp.bfloat16
HIGHEST = lax.Precision.HIGHEST


def mm(a, b):
    return jnp.dot(a, b, preferred_element_type=F32)


def lane_parts(v, heads):
    hi = v.astype(BF16)
    rest = v - hi.astype(F32)
    mid = rest.astype(BF16)
    lo = (rest - mid.astype(F32)).astype(BF16)
    lane = lax.broadcasted_iota(jnp.int32, v.shape, 1)
    return jnp.where(
        lane < heads, hi.astype(F32), jnp.where(lane < 2 * heads, mid.astype(F32), lo.astype(F32))
    ).astype(BF16)


def three(v):
    hi = v.astype(BF16).astype(F32)
    mid = (v - hi).astype(BF16).astype(F32)
    return hi, mid, v - hi - mid


def step_chunk(dt, k):
    part = dt[0, :, pl.ds(k * CHUNK, CHUNK)]
    fill = jnp.ones((128 - 3 * part.shape[0], CHUNK), F32)
    return jnp.concatenate([part, part, part, fill], axis=0).T


def total_rows(total, rows):
    hi, mid, lo = three(total)
    row = lax.broadcasted_iota(jnp.int32, (rows, EXTRA), 0)
    return jnp.where(
        row == 0, hi, jnp.where(row == 1, mid, jnp.where(row == 2, lo, 0.0))
    ).astype(BF16)


def tri_mask():
    rows = lax.broadcasted_iota(jnp.int32, (CHUNK, CHUNK), 0)
    cols = lax.broadcasted_iota(jnp.int32, (CHUNK, CHUNK), 1)
    return rows >= cols


def summary_kernel(groups, heads, me, x, b, dt, rate, spread, *rest):
    outs, (cum, parts, bt, st) = rest[:groups], rest[groups:]
    s, step = pl.program_id(0), pl.program_id(1)
    length = dt.shape[2]
    width = x.shape[2]
    rows = NSTATE // groups
    mine = pl.ds(pl.multiple_of(s * rows, rows), rows)

    @pl.when(step == 0)
    def _():
        tri = tri_mask().astype(F32)
        steps = [step_chunk(dt, k) for k in range(length // CHUNK)]
        before = jnp.zeros((1, 128), F32)
        for k in range(length // CHUNK):
            at = pl.ds(k * CHUNK, CHUNK)
            part = (
                jnp.dot(tri, steps[k] * rate[...], precision=HIGHEST, preferred_element_type=F32)
                + before
            )
            cum[0, at, :] = part
            before = part[CHUNK - 1 :, :]
            bt[:, at] = b[0, at, :].astype(F32).T.astype(BF16)
        for k in range(length // CHUNK):
            at = pl.ds(k * CHUNK, CHUNK)
            parts[at, :] = lane_parts(jnp.exp2(before - cum[0, at, :]) * steps[k], heads)
        extra = total_rows(before, rows)
        for d in range(groups):
            outs[d][mine, pl.ds(outs[d].shape[1] - EXTRA, EXTRA)] = extra

    for i in range(width // TILE):
        at = pl.ds(i * TILE, TILE)
        wide = spread[:, pl.ds(pl.multiple_of(step * width + i * TILE, TILE), TILE)]
        weighted = (x[0, :, at].astype(F32) * mm(parts[...], wide)).astype(BF16)
        st[:, at] = mm(bt[...], weighted)
    for d in range(groups):
        outs[d][mine, pl.ds(pl.multiple_of(step * width, 128), width)] = st[
            pl.ds(pl.multiple_of((me[0] ^ d) * rows, 8), rows), :
        ].astype(BF16)


def summary(me, x, b, dt, rate, spread, groups):
    count, length, feats = x.shape
    width = 1280
    heads = feats // HEAD_DIM
    piece = (count * NSTATE // groups, feats + EXTRA)
    return pl.pallas_call(
        functools.partial(summary_kernel, groups, heads),
        grid_spec=pltpu.PrefetchScalarGridSpec(
            num_scalar_prefetch=1,
            grid=(count, feats // width),
            in_specs=[
                pl.BlockSpec((1, length, width), lambda s, i, m: (s, 0, i)),
                pl.BlockSpec((1, length, NSTATE), lambda s, i, m: (s, 0, 0)),
                pl.BlockSpec((1, heads, length), lambda s, i, m: (s, 0, 0)),
                pl.BlockSpec((1, 128), lambda s, i, m: (0, 0)),
                pl.BlockSpec(memory_space=pltpu.VMEM),
            ],
            out_specs=[pl.BlockSpec(piece, lambda s, i, m: (0, 0))] * groups
            + [pl.BlockSpec((1, length, 128), lambda s, i, m: (s, 0, 0))],
            scratch_shapes=[
                pltpu.VMEM((length, 128), BF16),
                pltpu.VMEM((NSTATE, length), BF16),
                pltpu.VMEM((NSTATE, width), F32),
            ],
        ),
        out_shape=[jax.ShapeDtypeStruct(piece, BF16)] * groups
        + [jax.ShapeDtypeStruct((count, length, 128), F32)],
        compiler_params=pltpu.CompilerParams(vmem_limit_bytes=60 << 20),
        cost_estimate=pl.CostEstimate(flops=2_800_000_000, bytes_accessed=8_000_000, transcendentals=0),
        name="summary",
    )(me, x, b, dt, rate, spread)


def totals_of(views, feats):
    out = []
    for view in views:
        block = view[0:8, pl.ds(feats, EXTRA)].astype(F32)
        out.append(block[0:1] + block[1:2] + block[2:3])
    return out


def factors(totals, spread, heads, tile):
    fill = [jnp.zeros((1, 128), F32)] * (-len(totals) % 16)
    stacked = jnp.concatenate(totals + fill, axis=0)
    return mm(lane_parts(jnp.exp2(stacked), heads), spread[:, tile])


def plane_kernel(groups, heads, count, me, spread, *rest):
    pieces, (out, ordered) = rest[:groups], rest[-2:]
    feats = spread.shape[1]
    rows = out.shape[0] // count
    for d in range(groups):
        ordered[d] = pieces[d][...].astype(F32)
    for s in range(count):
        at_rows = pl.ds(s * rows, rows)
        views = [ordered.at[me[0] ^ p, at_rows, :] for p in range(groups)]
        totals = totals_of(views, feats)
        for i in range(feats // TILE):
            at = pl.ds(i * TILE, TILE)
            decay = factors(totals, spread, heads, at)
            total = views[0][:, at]
            for p in range(1, groups):
                total = decay[p : p + 1] * total + views[p][:, at]
            out[at_rows, at] = total.astype(BF16)
        out[at_rows, pl.ds(feats, EXTRA)] = total_rows(
            functools.reduce(lambda a, b: a + b, totals), rows
        )


def plane_total(me, spread, pieces, count, after):
    groups = len(pieces)
    rows, wide = pieces[0].shape
    heads = spread.shape[1] // HEAD_DIM
    vmem = pl.BlockSpec(memory_space=pltpu.VMEM)
    return pl.pallas_call(
        functools.partial(plane_kernel, groups, heads, count),
        in_specs=[pl.BlockSpec(memory_space=pltpu.SMEM)]
        + [vmem] * (groups + 1)
        + [pl.BlockSpec(memory_space=pl.ANY)] * len(after),
        out_specs=vmem,
        out_shape=jax.ShapeDtypeStruct((rows, wide), BF16),
        scratch_shapes=[pltpu.VMEM((groups, rows, wide), F32)],
        compiler_params=pltpu.CompilerParams(vmem_limit_bytes=12 << 20),
        cost_estimate=pl.CostEstimate(flops=10_000_000, bytes_accessed=1_500_000, transcendentals=0),
        name="plane_total",
    )(me, spread, *pieces, *after)


def incoming_kernel(groups, hops, heads, count, me, spread, *rest):
    pieces, below = rest[:groups], rest[groups : groups + hops]
    outs = rest[-groups - 2 : -2]
    ordered, results = rest[-2:]
    feats = spread.shape[1]
    rows = outs[0].shape[0] // count
    for d in range(groups):
        ordered[d] = pieces[d][...].astype(F32)
    for s in range(count):
        at_rows = pl.ds(s * rows, rows)
        views = [ordered.at[me[0] ^ p, at_rows, :] for p in range(groups)]
        under = [ref.at[at_rows, :] for ref in below]
        totals = totals_of(views, feats) + totals_of(under, feats)
        for i in range(feats // TILE):
            at = pl.ds(i * TILE, TILE)
            decay = factors(totals, spread, heads, at)
            state = jnp.zeros((rows, TILE), F32)
            for k in range(hops - 1, -1, -1):
                state = decay[groups + k : groups + k + 1] * state + under[k][:, at].astype(F32)
            for p in range(groups):
                results[me[0] ^ p, at_rows, at] = state
                if p < groups - 1:
                    state = decay[p : p + 1] * state + views[p][:, at]
    for d in range(groups):
        outs[d][...] = results[d].astype(BF16)


def incoming_states(me, spread, pieces, below, count, after):
    groups, hops = len(pieces), len(below)
    rows, wide = pieces[0].shape
    feats = spread.shape[1]
    vmem = pl.BlockSpec(memory_space=pltpu.VMEM)
    return pl.pallas_call(
        functools.partial(incoming_kernel, groups, hops, feats // HEAD_DIM, count),
        in_specs=[pl.BlockSpec(memory_space=pltpu.SMEM)]
        + [vmem] * (1 + groups + hops)
        + [pl.BlockSpec(memory_space=pl.ANY)] * len(after),
        out_specs=[vmem] * groups,
        out_shape=[jax.ShapeDtypeStruct((rows, feats), BF16)] * groups,
        scratch_shapes=[
            pltpu.VMEM((groups, rows, wide), F32),
            pltpu.VMEM((groups, rows, feats), F32),
        ],
        compiler_params=pltpu.CompilerParams(vmem_limit_bytes=14 << 20),
        cost_estimate=pl.CostEstimate(flops=10_000_000, bytes_accessed=2_500_000, transcendentals=0),
        name="incoming_states",
    )(me, spread, *pieces, *below, *after)


def local_kernel(heads, first_head, x, b, c, dt, rate, skip, spread, *rest):
    y, token, state, skip_wide = rest[-4:]
    step = pl.program_id(0)
    feats = x.shape[2]
    offset = first_head * HEAD_DIM

    @pl.when(step == 0)
    def _():
        state[...] = jnp.zeros_like(state)
        token[...] = jnp.zeros_like(token)
        for i in range(feats // TILE):
            at = pl.ds(i * TILE, TILE)
            skip_wide[:, at] = mm(
                lane_parts(jnp.broadcast_to(skip[...], (16, 128)), heads),
                spread[:, pl.ds(offset + i * TILE, TILE)],
            )[:8]

    keep = tri_mask()
    steps = step_chunk(dt, 0)
    cum = jnp.dot(
        keep.astype(F32), steps * rate[...], precision=HIGHEST, preferred_element_type=F32
    )
    from_row = (cum - jnp.log2(steps)).T
    b_in, c_out = b[0], c[0]
    scores = lax.dot_general(c_out, b_in, (((1,), (1,)), ((), ())), preferred_element_type=F32)
    b_t = b_in.astype(F32).T.astype(BF16)
    grow = lane_parts(jnp.exp2(cum), heads)
    fade = lane_parts(jnp.exp2(cum[CHUNK - 1 :, :] - cum) * steps, heads)
    first = lax.broadcasted_iota(jnp.int32, (CHUNK, 128), 1) < HEAD_DIM
    nothing = jnp.zeros((CHUNK, 128), BF16)

    def weights(h):
        return jnp.where(
            keep, scores * jnp.exp2(cum[:, h : h + 1] - from_row[h : h + 1, :]), 0.0
        ).astype(BF16)

    for i in range(feats // TILE):
        at = pl.ds(i * TILE, TILE)
        wide = spread[:, pl.ds(offset + i * TILE, TILE)]
        grow_wide = mm(grow, wide)
        fade_wide = mm(fade, wide)
        x_in = x[0, :, at]
        x_float = x_in.astype(F32)
        old = state[:, at]
        y_tile = mm(c_out, old.astype(BF16)) * grow_wide + skip_wide[0:1, at] * x_float
        near = []
        for j in range(TILE // 128):
            h = first_head + (i * TILE + j * 128) // HEAD_DIM
            pair = x_in[:, j * 128 : (j + 1) * 128]
            near.append(
                mm(
                    jnp.concatenate([weights(h), weights(h + 1)], axis=1),
                    jnp.concatenate(
                        [jnp.where(first, pair, nothing), jnp.where(first, nothing, pair)], axis=0
                    ),
                )
            )
        y[0, :, at] = (y_tile + jnp.concatenate(near, axis=1)).astype(BF16)
        state[:, at] = grow_wide[CHUNK - 1 :, :] * old + mm(b_t, (x_float * fade_wide).astype(BF16))


def local_part(s, part, parts, x, b, c, dt, rate, skip, spread, before, after):
    count, length, feats = x.shape[0], x.shape[1], x.shape[2] // parts
    heads = x.shape[2] // HEAD_DIM
    return pl.pallas_call(
        functools.partial(local_kernel, heads, part * feats // HEAD_DIM),
        grid=(length // CHUNK,),
        in_specs=[
            pl.BlockSpec((1, CHUNK, feats), lambda i: (s, i, part)),
            pl.BlockSpec((1, CHUNK, NSTATE), lambda i: (s, i, 0)),
            pl.BlockSpec((1, CHUNK, NSTATE), lambda i: (s, i, 0)),
            pl.BlockSpec((1, heads, CHUNK), lambda i: (s, 0, i)),
            pl.BlockSpec((1, 128), lambda i: (0, 0)),
            pl.BlockSpec((1, 128), lambda i: (0, 0)),
            pl.BlockSpec(memory_space=pltpu.VMEM),
        ]
        + [pl.BlockSpec(memory_space=pl.ANY)] * (len(before) + len(after)),
        out_specs=[
            pl.BlockSpec((1, CHUNK, feats), lambda i: (s, i, part)),
            pl.BlockSpec((8, 128), lambda i: (0, 0)),
        ],
        out_shape=[
            jax.ShapeDtypeStruct((count, length, feats * parts), BF16),
            jax.ShapeDtypeStruct((8, 128), F32),
        ],
        input_output_aliases={7: 0} if before else {},
        scratch_shapes=[pltpu.VMEM((NSTATE, feats), F32), pltpu.VMEM((8, feats), F32)],
        compiler_params=pltpu.CompilerParams(vmem_limit_bytes=60 << 20),
        cost_estimate=pl.CostEstimate(flops=6_000_000_000, bytes_accessed=9_000_000, transcendentals=0),
        name="local_part",
    )(x, b, c, dt, rate, skip, spread, *before, *after)


def gate_kernel(groups, heads, slots, me, *refs):
    pieces, refs = refs[:groups], refs[groups:]
    y, z, c, cum, gain, slot_pos, spread = refs[:7]
    gated, squares = refs[7:9]
    sends = refs[9 : 9 + groups]
    entering, routed = refs[9 + groups :]
    s, step = pl.program_id(0), pl.program_id(1)
    feats = spread.shape[1]
    rows = NSTATE // groups
    share = slots // groups
    row = s * pl.num_programs(1) + step

    @pl.when(step == 0)
    def _():
        mine = pl.ds(pl.multiple_of(s * rows, 8), rows)
        for d in range(groups):
            entering[pl.ds(pl.multiple_of((me[0] ^ d) * rows, 8), rows), :] = pieces[d][
                mine, :
            ].astype(F32)

    @pl.when(row == 0)
    def _():
        routed[...] = jnp.zeros_like(routed)

    for sub in range(z.shape[1] // CHUNK):
        now = pl.ds(sub * CHUNK, CHUNK)
        line = row * (z.shape[1] // CHUNK) + sub
        grow = lane_parts(jnp.exp2(cum[0, now, :]), heads)
        c_out = c[0, now, :]
        square = jnp.zeros((CHUNK, 128), F32)
        here = slot_pos[...] == line * CHUNK + lax.broadcasted_iota(jnp.int32, (slots, CHUNK), 1)
        pick = here.astype(F32).astype(BF16)
        for i in range(feats // TILE):
            at = pl.ds(i * TILE, TILE)
            far = mm(c_out, entering[:, at].astype(BF16)) * mm(grow, spread[:, at])
            half = z[0, now, at].astype(F32) * 0.5
            value = (y[0, now, at].astype(F32) + far) * (half + half * jnp.tanh(half))
            gated[0, now, at] = (value * gain[:, at]).astype(BF16)
            power = value * value
            for j in range(TILE // 128):
                square = square + power[:, j * 128 : (j + 1) * 128]
        wide = jnp.broadcast_to(jnp.sum(square, axis=1, keepdims=True), (CHUNK, 128))
        squares[pl.ds(line, 1), :] = wide.T[0:1, :]
        hi, mid, lo = three(wide)
        lane = lax.broadcasted_iota(jnp.int32, (CHUNK, EXTRA), 1)
        extra = jnp.where(lane == 0, hi, jnp.where(lane == 1, mid, jnp.where(lane == 2, lo, 0.0)))
        routed[:, pl.ds(0, feats)] += mm(pick, gated[0, now, :])
        routed[:, pl.ds(feats, EXTRA)] += mm(pick, extra.astype(BF16))

    @pl.when(row == pl.num_programs(0) * pl.num_programs(1) - 1)
    def _():
        for d in range(groups):
            sends[d][...] = routed[pl.ds(d * share, share), :].astype(BF16)


def gate(me, pieces, y, z, c, cum, gain, slot_pos, spread):
    count, length, feats = z.shape
    groups = len(pieces)
    slots = slot_pos.shape[0]
    fixed = lambda shape: pl.BlockSpec(shape, lambda s, i, m: (0,) * len(shape))
    block = lambda width: pl.BlockSpec((1, GATE_ROWS, width), lambda s, i, m: (s, i, 0))
    send = (slots // groups, feats + EXTRA)
    lines = (count * length // CHUNK, 128)
    return pl.pallas_call(
        functools.partial(gate_kernel, groups, feats // HEAD_DIM, slots),
        grid_spec=pltpu.PrefetchScalarGridSpec(
            num_scalar_prefetch=1,
            grid=(count, length // GATE_ROWS),
            in_specs=[fixed(pieces[0].shape)] * groups
            + [block(feats), block(feats), block(NSTATE), block(128)]
            + [fixed((1, feats)), fixed((slots, 1)), pl.BlockSpec(memory_space=pltpu.VMEM)],
            out_specs=[block(feats), fixed(lines)] + [fixed(send)] * groups,
            scratch_shapes=[
                pltpu.VMEM((NSTATE, feats), F32),
                pltpu.VMEM((slots, feats + EXTRA), F32),
            ],
        ),
        out_shape=[jax.ShapeDtypeStruct((count, length, feats), BF16), jax.ShapeDtypeStruct(lines, F32)]
        + [jax.ShapeDtypeStruct(send, BF16)] * groups,
        compiler_params=pltpu.CompilerParams(vmem_limit_bytes=40 << 20),
        cost_estimate=pl.CostEstimate(flops=2_000_000_000, bytes_accessed=20_000_000, transcendentals=0),
        name="gate",
    )(me, *pieces, y, z, c, cum, gain, slot_pos, spread)


def scale_kernel(gated, mine, other, *rest):
    out, token = rest[-2:]
    token[...] = jnp.zeros_like(token)
    row = pl.ds(pl.program_id(0) * pl.num_programs(1) + pl.program_id(1), 1)
    mean = (mine[row, :] + other[row, :]) / (HEAD_TOTAL * HEAD_DIM)
    inv = jnp.broadcast_to(lax.rsqrt(mean + norm_eps), (CHUNK, 128)).T
    for i in range(gated.shape[2] // 128):
        at = pl.ds(i * 128, 128)
        out[0, :, at] = (gated[0, :, at].astype(F32) * inv).astype(BF16)


def scale(gated, mine, other, after):
    count, length, feats = gated.shape
    fixed = lambda shape: pl.BlockSpec(shape, lambda s, i: (0,) * len(shape))
    block = pl.BlockSpec((1, CHUNK, feats), lambda s, i: (s, i, 0))
    return pl.pallas_call(
        scale_kernel,
        grid=(count, length // CHUNK),
        in_specs=[block, fixed(mine.shape), fixed(mine.shape)]
        + [pl.BlockSpec(memory_space=pl.ANY)] * len(after),
        out_specs=[block, fixed((8, 128))],
        out_shape=[jax.ShapeDtypeStruct(gated.shape, BF16), jax.ShapeDtypeStruct((8, 128), F32)],
        compiler_params=pltpu.CompilerParams(vmem_limit_bytes=10 << 20),
        cost_estimate=pl.CostEstimate(flops=10_000_000, bytes_accessed=8_000_000, transcendentals=0),
        name="scale",
    )(gated, mine, other, *after)


def join_kernel(count, *refs):
    out = refs[-1]
    share = refs[0].shape[0]
    for k in range(count):
        out[pl.ds(k * share, share), :] = refs[k][...]


def join(parts, after):
    share, wide = parts[0].shape
    vmem = pl.BlockSpec(memory_space=pltpu.VMEM)
    return pl.pallas_call(
        functools.partial(join_kernel, len(parts)),
        in_specs=[vmem] * len(parts) + [pl.BlockSpec(memory_space=pl.ANY)] * len(after),
        out_specs=vmem,
        out_shape=jax.ShapeDtypeStruct((len(parts) * share, wide), BF16),
        compiler_params=pltpu.CompilerParams(vmem_limit_bytes=10 << 20),
        cost_estimate=pl.CostEstimate(flops=1_000_000, bytes_accessed=700_000, transcendentals=0),
        name="join",
    )(*parts, *after)


def expert_kernel(core, own, other, w1, b1, w2, *outs):
    feats = own.shape[1] - EXTRA
    share = outs[0].shape[0]
    sums = jnp.zeros((own.shape[0], 1), F32)
    for ref in (own, other):
        part = ref[:, pl.ds(feats, EXTRA)].astype(F32)
        lane = lax.broadcasted_iota(jnp.int32, part.shape, 1)
        sums = sums + jnp.sum(jnp.where(lane < 3, part, 0.0), axis=1, keepdims=True)
    inv = lax.rsqrt(sums / (HEAD_TOTAL * HEAD_DIM) + norm_eps)
    lower = pl.ds(pl.multiple_of(core[0] * feats, 128), feats)
    upper = pl.ds(pl.multiple_of((1 - core[0]) * feats, 128), feats)
    pre = mm(own[:, pl.ds(0, feats)], w1[0, lower, :]) + mm(
        other[:, pl.ds(0, feats)], w1[0, upper, :]
    )
    pre = pre * inv + b1[...]
    hidden = jax.nn.gelu(pre).astype(BF16).astype(F32)
    value = jnp.sum(hidden * w2[...].astype(F32), axis=1, keepdims=True)
    value = jnp.broadcast_to(value, (own.shape[0], 128))
    for k, out in enumerate(outs):
        out[...] = value[k * share : (k + 1) * share]


def expert(core, own, other, w1, b1, w2, count):
    share = own.shape[0] // count
    vmem = pl.BlockSpec(memory_space=pltpu.VMEM)
    return pl.pallas_call(
        expert_kernel,
        in_specs=[pl.BlockSpec(memory_space=pltpu.SMEM)] + [vmem] * 5,
        out_specs=[vmem] * count,
        out_shape=[jax.ShapeDtypeStruct((share, 128), F32)] * count,
        compiler_params=pltpu.CompilerParams(vmem_limit_bytes=14 << 20),
        cost_estimate=pl.CostEstimate(flops=400_000_000, bytes_accessed=6_000_000, transcendentals=0),
        name="expert",
    )(core, own, other, w1, b1, w2)


def body(
    x_inner,
    z_gate,
    b_input,
    c_output,
    step_sizes,
    decay_log,
    skip_gain,
    norm_gain,
    goal_pos,
    goal_owner,
    value_w1,
    value_b1,
    value_w2,
):
    count, length, feats = x_inner.shape
    heads = step_sizes.shape[2]
    devices = lax.axis_size("seq")
    planes = PLANES
    groups = devices // planes
    index = lax.axis_index("seq")
    place, plane = index % groups, index // groups
    me = place.reshape(1).astype(jnp.int32)
    core = lax.axis_index("head").reshape(1).astype(jnp.int32)

    def permute(value, where):
        return lax.ppermute(value, "seq", where)

    def across(value, d):
        return permute(value, [(i, i ^ d) for i in range(devices)])

    def swap(value):
        return lax.ppermute(value, "head", [(0, 1), (1, 0)])

    def triple(v, fill):
        return jnp.concatenate(
            [v, v, v, jnp.full(v.shape[:-1] + (128 - 3 * heads,), fill, F32)], axis=-1
        )

    lanes = np.arange(128)
    spread = jnp.asarray(
        (lanes[:, None] % heads == np.arange(feats)[None, :] // HEAD_DIM)
        & (lanes[:, None] < 3 * heads),
        BF16,
    )
    dt = jnp.swapaxes(step_sizes, 1, 2)
    rate = triple(-jnp.exp(decay_log) * LOG2E, 0.0)[None]
    skip = triple(skip_gain, 0.0)[None]
    gain = norm_gain[None]

    goal_dev = goal_pos.shape[1]
    owners = goal_owner.reshape(-1)
    positions = (
        goal_pos - index * length + length * jnp.arange(count, dtype=jnp.int32)[:, None]
    ).reshape(-1)
    ids = jnp.arange(owners.shape[0])
    same = (owners[:, None] == owners[None, :]) & (ids[None, :] < ids[:, None])
    rank = jnp.sum(same.astype(jnp.int32), axis=1)
    slot = (((owners % groups) ^ place) * planes + ((owners // groups) ^ plane)) * CAP + rank
    slots = devices * CAP
    taken = jnp.arange(slots)[:, None] == slot[None, :]
    slot_pos = jnp.max(jnp.where(taken, positions[None, :], -1), axis=1, keepdims=True)

    nothing = jnp.zeros((1,), jnp.int32)

    def upward(value, hops):
        hop = hops * groups
        return permute(value, [(i, i + hop) for i in range(devices - hop)])

    def local(s, part, parts, before, after):
        return local_part(
            s, part, parts, x_inner, b_input, c_output, dt, rate, skip, spread, before, after
        )

    def spread_out(own):
        return [own[0]] + [across(own[d], d) for d in range(1, groups)]

    *own, cum = summary(me, x_inner, b_input, dt, rate, spread, groups)
    gathered = spread_out(own)
    y, token = local(0, 0, 1, (), (own[0],))
    total = plane_total(me, spread, gathered, count, (token,))
    one = upward(total, 1)
    y, token = local(1, 0, 2, (y,), (total,))
    pair = plane_total(nothing, spread, [one, total], count, (token,))
    two = upward(pair, 2)
    y, token = local(1, 1, 2, (y,), (pair,))
    entering = spread_out(incoming_states(me, spread, gathered, [one, two], count, (token,)))
    gated, mine, *sends = gate(
        me, entering, y, z_gate, c_output, cum, gain, slot_pos, spread
    )
    near = spread_out(sends)
    far = [
        jnp.concatenate([v[k * CAP : (k + 1) * CAP] for v in near], axis=0) for k in range(planes)
    ]
    own = [far[0]] + [across(far[k], k * groups) for k in range(1, planes)]
    layer_out, token = scale(gated, mine, swap(mine), (far[1],))
    rows = join(own, (token,))
    answers = expert(core, rows, swap(rows), value_w1, value_b1, value_w2, planes)
    answers = [v[:, :1] for v in answers]
    back = [answers[0]] + [across(answers[k], k * groups) for k in range(1, planes)]
    table = jnp.concatenate(back, axis=1)
    table = table + swap(table)
    tables = [table] + [across(table, d) for d in range(1, groups)]
    flat = jnp.concatenate(
        [t[d * CAP : (d + 1) * CAP].T.reshape(-1) for d, t in enumerate(tables)]
    )
    values = jnp.sum(jnp.where(taken, flat[:, None], 0.0), axis=0).reshape(count, goal_dev)
    return (layer_out, values)


def solution(mesh):
    placed = (
        P(None, "seq", "head"),
        P(None, "seq", "head"),
        P(None, "seq", None),
        P(None, "seq", None),
        P(None, "seq", "head"),
        P("head"),
        P("head"),
        P("head"),
        P(None, "seq"),
        P(None, "seq"),
        P("seq", None, "head"),
        P("seq", "head"),
        P("seq", "head"),
    )
    return jax.shard_map(
        body,
        mesh=mesh,
        in_specs=placed,
        out_specs=(P(None, "seq", "head"), P(None, "seq")),
        check_vma=False,
    )
```
